32 devices in a mesh: dp: 8 (over z, x), cent: 4 (over y, core).
Axes of the slice: x: 2, y: 2, z: 4, core: 2. Of those that a mesh axis runs over, the one named last changes fastest.
Arguments:
- embeddings: bfloat16 [8192, 512], P('dp'), may hold values from -60 to 60, as said below
- centroids: bfloat16 [16384, 512], P('cent'), may hold values from -60 to 60, as said below
Outputs:
- new_centroids: float32 [16384, 512], P(('cent', 'dp'))
- column_mass: float32 [16384], P(('cent', 'dp'))
The draws below stay inside these ranges and needn't reach their ends.
Inputs may be any that keep to these rules, and one draw needn't show every extreme that they name: `embeddings`: every row is nonzero. `centroids`: every row is nonzero.
All inputs are finite; a program needn't handle non-finite values.
Results may differ from the reference program's by a relative error of at most 0.00074.
Values sent between devices are 32-bit elements; how exact they have to be, the bound alone decides.
A program may use at most 128 MiB of HBM per device.

```python
import math
import jax
import jax.numpy as jnp
from jax import lax

D = 512
K = 16384
ROWS_DEV = 1024
ITERS = 3
ROWS = 8192
N_DP = 8


def cluster_directions(key, width):
    common = jax.random.fold_in(key, 5)
    return jnp.clip(jax.random.normal(common, (8, width), jnp.float32), -4.0, 4.0)


def cluster_members(key, salt, count):
    first, second = jax.random.split(jax.random.fold_in(key, salt))
    cluster_order = jax.random.permutation(first, 8)
    ticket = jax.random.randint(second, (count,), 0, 36)
    bucket_edges = jnp.array([1, 3, 6, 10, 15, 21, 28], jnp.int32)
    bucket = jnp.sum((ticket[:, None] >= bucket_edges[None, :]).astype(jnp.int32), axis=1)
    return jnp.take(cluster_order, bucket, axis=0)


def scaled_rows(key, salt, count, width):
    directions = cluster_directions(key, width)
    members = cluster_members(key, salt + 1, count)
    first, second, third = jax.random.split(jax.random.fold_in(key, salt), 3)
    row_scale = jnp.exp(jax.random.uniform(second, (count, 1), jnp.float32, 0.0, math.log(10.0)))
    strength = jax.random.uniform(third, (count, 1), jnp.float32, 0.5, 1.0)
    noise_part = jnp.clip(jax.random.normal(first, (count, width), jnp.float32), -5.0, 5.0)
    picked = jnp.take(directions, members, axis=0)
    return jnp.clip(noise_part + strength * picked, -6.0, 6.0) * row_scale


def draw_embeddings(key, part):
    return scaled_rows(key, 11, ROWS, D).astype(jnp.bfloat16)


def draw_centroids(key, part):
    return scaled_rows(key, 23, K, D).astype(jnp.bfloat16)


def setup_inputs(seed: int = 0) -> dict:
    arg_keys = jax.random.split(jax.random.key(seed), 3)
    return {
        "embeddings": draw_embeddings(jax.random.fold_in(arg_keys[2], 71), 0),
        "centroids": draw_centroids(jax.random.fold_in(arg_keys[2], 71), 0),
    }


TAU = 0.02

def rms_rows(values):
    wide = values.astype(jnp.float32)
    return (wide * lax.rsqrt(lax.optimization_barrier(jnp.mean(wide * wide, axis=1, keepdims=True)) + 1e-06)).astype(jnp.bfloat16)

def energy_block(rows_block, cent_rows):
    scores = lax.dot_general(rows_block, cent_rows, (((1,), (1,)), ((), ())), preferred_element_type=jnp.float32)
    return jnp.exp(scores * (1.0 / (TAU * D)))

def reference(embeddings, centroids):
    high = lax.Precision.HIGHEST
    xh = rms_rows(embeddings)
    ch = rms_rows(centroids)
    blocks = xh.reshape(N_DP, ROWS_DEV, D)
    ratio = float(ROWS) / float(K)

    def sums(u, v):

        def step(carry, item):
            block, weights = item
            energy = energy_block(block, ch)
            rows_sum = jnp.dot(energy, v, precision=high)
            return (carry + jnp.dot(weights, energy, precision=high), rows_sum)
        cols, rows_sum = lax.scan(step, jnp.zeros((K,), jnp.float32), (blocks, u.reshape(N_DP, ROWS_DEV)))
        return (rows_sum.reshape(ROWS), cols)
    u = jnp.ones((ROWS,), jnp.float32)
    v = jnp.ones((K,), jnp.float32)
    for step_index in range(ITERS):
        rows_sum, cols = sums(u, v)
        u, v = (jnp.sqrt(u / rows_sum), jnp.sqrt(v * ratio / cols))

    def final_step(carry, item):
        cols, weighted = carry
        block, weights = item
        energy = energy_block(block, ch)
        cols = cols + jnp.dot(weights, energy, precision=high)
        plan = (float(K) * weights[:, None] * energy * v[None, :]).astype(jnp.bfloat16)
        weighted = weighted + lax.dot_general(plan, block, (((0,), (0,)), ((), ())), preferred_element_type=jnp.float32)
        return ((cols, weighted), None)
    init = (jnp.zeros((K,), jnp.float32), jnp.zeros((K, D), jnp.float32))
    (cols, weighted), unused = lax.scan(final_step, init, (blocks, u.reshape(N_DP, ROWS_DEV)))
    column_mass = v * cols * (float(K) / float(ROWS))
    new_centroids = weighted * lax.rsqrt(lax.optimization_barrier(jnp.mean(weighted * weighted, axis=1, keepdims=True)) + 1e-06)
    return (new_centroids, column_mass)
```

```python
import functools
import jax
import jax.numpy as jnp
from jax import lax
from jax.experimental import pallas as pl
from jax.experimental.pallas import tpu as pltpu
from jax.sharding import PartitionSpec as P

ITERS = 3
TAU = 0.02
MESH = pl.DeviceIdType.MESH
NT = (((1,), (1,)), ((), ()))
NB = 8
CHUNK = 256


def rms_rows(values):
    wide = values.astype(jnp.float32)
    return (wide * lax.rsqrt(jnp.mean(wide * wide, axis=1, keepdims=True) + 1e-06)).astype(
        jnp.bfloat16
    )


def lane_tiles(values):
    total = values[:, :128]
    for t in range(1, values.shape[1] // 128):
        total = total + values[:, t * 128 : (t + 1) * 128]
    return total


def to_column(row):
    return jnp.broadcast_to(row, (128, row.shape[1])).T


def to_row(tile):
    return jnp.sum(tile.T, axis=0, keepdims=True)


def kernel(
    total_rows, total_cents, n_dp, n_cent,
    emb, cent, out_w, out_m,
    energy, ch, xg, xb, ucol, racc, cr, rr, uz, vv, ws, wr, cfs, cfr,
    c_send, c_recv, r_send, r_recv, z_send, z_recv, y_send, y_recv, k_send, k_recv,
    u_send, u_recv, w_send, w_recv,
):
    n_z = n_dp // 2
    rows, width = emb.shape
    cents = cent.shape[0]
    block = cents // NB
    quarter = rows // n_cent
    scale = 1.0 / (TAU * width)
    ratio = total_rows / total_cents
    d = lax.axis_index("dp")
    c = lax.axis_index("cent")
    z, x = d // 2, lax.rem(d, 2)
    y, core = c // 2, lax.rem(c, 2)
    dp_peers = [lax.rem(d + k, n_dp) for k in range(1, n_dp)]
    c_peers = [lax.rem(c + k, n_cent) for k in range(1, n_cent)]
    z_peers = [lax.rem(z + k, n_z) for k in range(1, n_z)]
    c_y = (1 - y) * 2 + core
    c_core = y * 2 + (1 - core)
    c_far = (1 - y) * 2 + (1 - core)
    d_x = z * 2 + (1 - x)

    barrier = pltpu.get_barrier_semaphore()
    for peer in dp_peers:
        pl.semaphore_signal(barrier, inc=1, device_id={"dp": peer, "cent": c}, device_id_type=MESH)
    for peer in c_peers:
        pl.semaphore_signal(barrier, inc=1, device_id={"dp": d, "cent": peer}, device_id_type=MESH)
    pl.semaphore_wait(barrier, n_dp - 1 + n_cent - 1)

    def remote(src, dst, ssem, rsem, dp, cn):
        return pltpu.make_async_remote_copy(
            src_ref=src, dst_ref=dst, send_sem=ssem, recv_sem=rsem,
            device_id={"dp": dp, "cent": cn}, device_id_type=MESH,
        )

    mine = pl.multiple_of(c * quarter, quarter)
    xg[z, c] = rms_rows(emb[pl.ds(mine, quarter), :]).astype(jnp.float32)

    def z_copy(k):
        return remote(
            xg.at[z, c], xg.at[z, c], z_send.at[k], z_recv.at[z], z_peers[k] * 2 + x, c
        )

    def z_arrival(k):
        src = z_peers[k]
        return remote(xg.at[src, c], xg.at[src, c], z_send.at[k], z_recv.at[src], d, c_y)

    def y_copy(k):
        src = z_peers[k]
        return remote(xg.at[src, c], xg.at[src, c], y_send.at[k], y_recv.at[src], d, c_y)

    def y_arrival(k):
        src = z_peers[k]
        return remote(xg.at[src, c_y], xg.at[src, c_y], y_send.at[k], y_recv.at[src], d, c_y)

    def k_copy(k, s, who):
        src = z_peers[k]
        return remote(
            xg.at[src, who], xg.at[src, who], k_send.at[k, s], k_recv.at[src, s], d, c_core
        )

    for k in range(n_z - 1):
        z_copy(k).start()

    base = pl.multiple_of(z * rows, rows)
    for i in range(n_cent):
        xb[pl.ds(base + i * quarter, quarter), :] = rms_rows(emb[i * quarter : (i + 1) * quarter, :])

    def exchange(it):
        rr[it, c] = to_row(racc[...])
        for k, peer in enumerate(dp_peers):
            remote(cr.at[it, d], cr.at[it, d], c_send.at[it, k], c_recv.at[it, d], peer, c).start()
        for k, peer in enumerate(c_peers):
            remote(rr.at[it, c], rr.at[it, c], r_send.at[it, k], r_recv.at[it, c], d, peer).start()
        for k, peer in enumerate(c_peers):
            got = remote(
                rr.at[it, peer], rr.at[it, peer], r_send.at[it, k], r_recv.at[it, peer], d, peer
            )
            got.wait()
        row_sum = rr[it, 0]
        for k in range(1, n_cent):
            row_sum = row_sum + rr[it, k]
        u_old = uz[z] if it else jnp.ones((1, rows), jnp.float32)
        u_new = jnp.sqrt(u_old / row_sum)
        uz[z] = u_new
        if it < ITERS - 1:
            ucol[...] = to_column(u_new)
        for k, peer in enumerate(dp_peers):
            got = remote(
                cr.at[it, peer], cr.at[it, peer], c_send.at[it, k], c_recv.at[it, peer], peer, c
            )
            got.wait()
        col_sum = cr[it, 0]
        for k in range(1, n_dp):
            col_sum = col_sum + cr[it, k]
        v_old = vv[...] if it else jnp.ones((NB, block), jnp.float32)
        vv[...] = jnp.sqrt(v_old * ratio / col_sum)

    racc[...] = jnp.zeros_like(racc)

    @pl.loop(0, NB)
    def _(b):
        at = pl.multiple_of(b * block, block)
        ch_b = rms_rows(cent[pl.ds(at, block), :])
        ch[pl.ds(at, block), :] = ch_b
        col = jnp.zeros((8, block), jnp.float32)
        for i in range(n_cent):
            part = slice(i * quarter, (i + 1) * quarter)
            s = lax.dot_general(
                xb[pl.ds(base + i * quarter, quarter), :], ch_b, NT,
                preferred_element_type=jnp.float32,
            )
            e = jnp.exp(s * scale)
            energy[b, part, :] = e
            racc[part, :] += lane_tiles(e)
            col = col + jnp.sum(e.reshape(quarter // 8, 8, block), axis=0)
        cr[0, d, pl.ds(b, 1), :] = jnp.sum(col, axis=0, keepdims=True)

    exchange(0)

    group = 64
    for it in range(1, ITERS):
        racc[...] = jnp.zeros_like(racc)

        @pl.loop(0, NB)
        def _(b):
            v_b = jnp.broadcast_to(vv[pl.ds(b, 1), :], (8, block))

            def step(g, col):
                r0 = pl.multiple_of(g * group, group)
                for i in range(group // 8):
                    e = energy[b, pl.ds(r0 + i * 8, 8), :]
                    u8 = ucol[pl.ds(r0 + i * 8, 8), :]
                    col = col + e * jnp.concatenate([u8] * (block // 128), axis=1)
                    racc[pl.ds(r0 + i * 8, 8), :] += lane_tiles(e * v_b)
                return col

            col = lax.fori_loop(0, rows // group, step, jnp.zeros((8, block), jnp.float32))
            cr[it, d, pl.ds(b, 1), :] = jnp.sum(col, axis=0, keepdims=True)

        exchange(it)

    def u_copy(k, owner):
        return remote(
            uz.at[owner], uz.at[owner], u_send.at[k], u_recv.at[owner], z_peers[k] * 2 + x, c
        )

    for k in range(n_z - 1):
        u_copy(k, z).start()
    for k in range(n_z - 1):
        z_copy(k).wait_send()
        z_arrival(k).wait_recv()
        y_copy(k).start()
        k_copy(k, 0, c).start()
    for k in range(n_z - 1):
        y_arrival(k).wait()
        k_copy(k, 1, c_y).start()
    for k in range(n_z - 1):
        k_copy(k, 0, c_core).wait()
        k_copy(k, 1, c_far).wait()
        u_copy(k, z_peers[k]).wait()
        src = z_peers[k]
        for i in range(n_cent):
            xb[pl.ds(pl.multiple_of(src * rows + i * quarter, quarter), quarter), :] = xg[
                src, i
            ].astype(jnp.bfloat16)

    def weigh(owner, s, dst):
        at = pl.multiple_of(owner * block + s * CHUNK, CHUNK)
        cc = ch[pl.ds(at, CHUNK), :]
        v_col = to_column(vv[pl.ds(owner, 1), :][:, s * CHUNK : (s + 1) * CHUNK])
        v_tile = jnp.concatenate([v_col] * (block // 128), axis=1)
        dst[s] = jnp.zeros((CHUNK, width), jnp.float32)

        def step(zz, acc):
            for h in range(rows // block):
                xr = xb[pl.ds(pl.multiple_of(zz * rows + h * block, block), block), :]
                u = uz[zz][:, h * block : (h + 1) * block]
                e = jnp.exp(
                    lax.dot_general(cc, xr, NT, preferred_element_type=jnp.float32) * scale
                )
                acc = acc + lane_tiles(e * u)
                q = ((total_cents * u) * e * v_tile).astype(jnp.bfloat16)
                dst[s] += jnp.dot(q, xr, preferred_element_type=jnp.float32)
            return acc

        acc = lax.fori_loop(0, n_z, step, jnp.zeros((CHUNK, 128), jnp.float32))
        return to_row(acc)

    n_s = block // CHUNK

    def w_copy(s):
        return remote(ws.at[s], wr.at[s], w_send.at[s], w_recv.at[s], d_x, c)

    for s in range(n_s):
        cfs[:, s * CHUNK : (s + 1) * CHUNK] = weigh(d_x, s, ws)
        w_copy(s).start()
    cf_copy = remote(cfs, cfr, w_send.at[n_s], w_recv.at[n_s], d_x, c)
    cf_copy.start()
    for s in range(n_s):
        out_m[:, s * CHUNK : (s + 1) * CHUNK] = weigh(d, s, out_w)
    for s in range(n_s):
        w_copy(s).wait()
        w = out_w[s] + wr[s]
        out_w[s] = w * lax.rsqrt(jnp.mean(w * w, axis=1, keepdims=True) + 1e-06)
    cf_copy.wait()
    out_m[...] = vv[pl.ds(d, 1), :] * (out_m[...] + cfr[...]) * (total_cents / total_rows)


def fused(embeddings, centroids):
    n_dp, n_cent = lax.axis_size("dp"), lax.axis_size("cent")
    rows, width = embeddings.shape
    cents = centroids.shape[0]
    n_z = n_dp // 2
    block = cents // NB
    quarter = rows // n_cent
    n_s = block // CHUNK
    f32 = jnp.float32
    dma = pltpu.SemaphoreType.DMA
    w, m = pl.pallas_call(
        functools.partial(
            kernel, float(rows * n_dp), float(cents * n_cent), n_dp, n_cent
        ),
        out_shape=(
            jax.ShapeDtypeStruct((n_s, CHUNK, width), f32),
            jax.ShapeDtypeStruct((1, block), f32),
        ),
        in_specs=[pl.BlockSpec(memory_space=pltpu.VMEM)] * 2,
        out_specs=(pl.BlockSpec(memory_space=pltpu.VMEM),) * 2,
        scratch_shapes=[
            pltpu.VMEM((NB, rows, block), f32),
            pltpu.VMEM((cents, width), jnp.bfloat16),
            pltpu.VMEM((n_z, n_cent, quarter, width), f32),
            pltpu.VMEM((n_z * rows, width), jnp.bfloat16),
            pltpu.VMEM((rows, 128), f32),
            pltpu.VMEM((rows, 128), f32),
            pltpu.VMEM((ITERS, n_dp, NB, block), f32),
            pltpu.VMEM((ITERS, n_cent, 1, rows), f32),
            pltpu.VMEM((n_z, 1, rows), f32),
            pltpu.VMEM((NB, block), f32),
            pltpu.VMEM((n_s, CHUNK, width), f32),
            pltpu.VMEM((n_s, CHUNK, width), f32),
            pltpu.VMEM((1, block), f32),
            pltpu.VMEM((1, block), f32),
            dma((ITERS, n_dp - 1)),
            dma((ITERS, n_dp)),
            dma((ITERS, n_cent - 1)),
            dma((ITERS, n_cent)),
            dma((n_z - 1,)),
            dma((n_z,)),
            dma((n_z - 1,)),
            dma((n_z,)),
            dma((n_z - 1, 2)),
            dma((n_z, 2)),
            dma((n_z - 1,)),
            dma((n_z,)),
            dma((n_s + 1,)),
            dma((n_s + 1,)),
        ],
        compiler_params=pltpu.CompilerParams(
            collective_id=0, has_side_effects=True, vmem_limit_bytes=60 * 2**20
        ),
    )(embeddings, centroids)
    return w.reshape(block, width), m.reshape(block)


def column_total(weights, energy):
    return lax.psum(jnp.dot(weights, energy, precision=lax.Precision.HIGHEST), "dp")


def local(embeddings, centroids):
    n_data = lax.axis_size("dp")
    xh = rms_rows(embeddings)
    ch = rms_rows(centroids)
    local_rows, width = xh.shape
    local_cents = ch.shape[0]
    total_rows = float(local_rows * n_data)
    total_cents = float(local_cents * lax.axis_size("cent"))
    scores = lax.dot_general(xh, ch, NT, preferred_element_type=jnp.float32)
    energy = jnp.exp(scores * (1.0 / (TAU * width)))
    u = jnp.ones((local_rows,), jnp.float32)
    v = jnp.ones((local_cents,), jnp.float32)
    for step_index in range(ITERS):
        rows_sum = lax.psum(jnp.dot(energy, v, precision=lax.Precision.HIGHEST), "cent")
        cols = column_total(u, energy)
        u, v = (jnp.sqrt(u / rows_sum), jnp.sqrt(v * (total_rows / total_cents) / cols))
    cols = column_total(u, energy)
    plan = (total_cents * u[:, None] * energy * v[None, :]).astype(jnp.bfloat16)
    share = local_cents // n_data
    weighted = lax.dot_general(
        plan, xh, (((0,), (0,)), ((), ())), preferred_element_type=jnp.float32
    )
    mine = lax.psum_scatter(weighted, "dp", scatter_dimension=0, tiled=True)
    mass_all = v * cols * (total_cents / total_rows)
    column_mass = lax.dynamic_slice_in_dim(mass_all, lax.axis_index("dp") * share, share, 0)
    new_centroids = mine * lax.rsqrt(jnp.mean(mine * mine, axis=1, keepdims=True) + 1e-06)
    return (new_centroids, column_mass)


def solution(mesh):
    in_specs = (P("dp", None), P("cent", None))
    out_specs = (P(("cent", "dp"), None), P(("cent", "dp")))
    small = mesh.shape["dp"] == NB and mesh.shape["cent"] == 4
    body = fused if small else local
    return jax.shard_map(body, mesh=mesh, in_specs=in_specs, out_specs=out_specs, check_vma=False)
```

```python
import functools
import jax
import jax.numpy as jnp
from jax import lax
from jax.experimental import pallas as pl
from jax.experimental.pallas import tpu as pltpu
from jax.sharding import PartitionSpec as P

ITERS = 3
TAU = 0.02
MESH = pl.DeviceIdType.MESH
NT = (((1,), (1,)), ((), ()))
NB = 8
CHUNK = 256


def rms_rows(values):
    wide = values.astype(jnp.float32)
    return (wide * lax.rsqrt(jnp.mean(wide * wide, axis=1, keepdims=True) + 1e-06)).astype(
        jnp.bfloat16
    )


def lane_tiles(values):
    total = values[:, :128]
    for t in range(1, values.shape[1] // 128):
        total = total + values[:, t * 128 : (t + 1) * 128]
    return total


def to_column(row):
    return jnp.broadcast_to(row, (128, row.shape[1])).T


def to_row(tile):
    return jnp.sum(tile.T, axis=0, keepdims=True)


def kernel(
    total_rows, total_cents, n_dp, n_cent,
    emb, cent, out_w, out_m,
    energy, ch, xg, xb, ucol, racc, cr, rr, uz, vv, ws, wr, cfs, cfr,
    c_send, c_recv, r_send, r_recv, z_send, z_recv, y_send, y_recv, k_send, k_recv,
    u_send, u_recv, w_send, w_recv,
):
    n_z = n_dp // 2
    rows, width = emb.shape
    cents = cent.shape[0]
    block = cents // NB
    quarter = rows // n_cent
    scale = 1.0 / (TAU * width)
    ratio = total_rows / total_cents
    d = lax.axis_index("dp")
    c = lax.axis_index("cent")
    z, x = d // 2, lax.rem(d, 2)
    y, core = c // 2, lax.rem(c, 2)
    dp_peers = [lax.rem(d + k, n_dp) for k in range(1, n_dp)]
    c_peers = [lax.rem(c + k, n_cent) for k in range(1, n_cent)]
    z_peers = [lax.rem(z + k, n_z) for k in range(1, n_z)]
    c_y = (1 - y) * 2 + core
    c_core = y * 2 + (1 - core)
    c_far = (1 - y) * 2 + (1 - core)
    d_x = z * 2 + (1 - x)

    barrier = pltpu.get_barrier_semaphore()
    for peer in dp_peers:
        pl.semaphore_signal(barrier, inc=1, device_id={"dp": peer, "cent": c}, device_id_type=MESH)
    for peer in c_peers:
        pl.semaphore_signal(barrier, inc=1, device_id={"dp": d, "cent": peer}, device_id_type=MESH)
    pl.semaphore_wait(barrier, n_dp - 1 + n_cent - 1)

    def remote(src, dst, ssem, rsem, dp, cn):
        return pltpu.make_async_remote_copy(
            src_ref=src, dst_ref=dst, send_sem=ssem, recv_sem=rsem,
            device_id={"dp": dp, "cent": cn}, device_id_type=MESH,
        )

    mine = pl.multiple_of(c * quarter, quarter)
    xg[z, c] = rms_rows(emb[pl.ds(mine, quarter), :]).astype(jnp.float32)

    low = z // 2
    first = z + 1 - 2 * low
    last = 3 - 3 * low
    order = [first, 6 - z - first - last, last]
    middle = (z == 1) | (z == 2)

    def z_copy(src, to, sem):
        return remote(
            xg.at[src, c], xg.at[src, c], z_send.at[sem], z_recv.at[src], to * 2 + x, c
        )

    def z_arrival(src):
        z_copy(src, first, 0).wait_recv()

    def relay(src):
        to = jnp.where(src > z, z - 1, z + 1)
        return z_copy(src, to, src)

    def y_copy(src, who):
        return remote(xg.at[src, who], xg.at[src, who], y_send.at[src], y_recv.at[src], d, c_y)

    def k_copy(src, s, who):
        return remote(
            xg.at[src, who], xg.at[src, who], k_send.at[src, s], k_recv.at[src, s], d, c_core
        )

    def forward(j):
        if j == 0:
            z_arrival(order[0])

            @pl.when(middle)
            def _():
                relay(order[0]).start()
                z_arrival(order[1])
                relay(order[1]).start()

        if j == 1:

            @pl.when(jnp.logical_not(middle))
            def _():
                z_arrival(order[1])

        if j == 2:

            @pl.when(jnp.logical_not(middle))
            def _():
                z_arrival(order[2])

        if j < 3:
            y_copy(order[j], c).start()
            k_copy(order[j], 0, c).start()
        if j == 1:

            @pl.when(middle)
            def _():
                z_arrival(order[2])
                relay(order[2]).start()

        if j > 0:
            y_copy(order[j - 1], c_y).wait()
            k_copy(order[j - 1], 1, c_y).start()

    z_copy(z, first, z).start()

    @pl.when(middle)
    def _():
        z_copy(z, 2 * z - first, n_z).start()

    base = pl.multiple_of(z * rows, rows)
    for i in range(n_cent):
        xb[pl.ds(base + i * quarter, quarter), :] = rms_rows(emb[i * quarter : (i + 1) * quarter, :])

    def exchange(it):
        rr[it, c] = to_row(racc[...])
        for k, peer in enumerate(dp_peers):
            remote(cr.at[it, d], cr.at[it, d], c_send.at[it, k], c_recv.at[it, d], peer, c).start()
        for k, peer in enumerate(c_peers):
            remote(rr.at[it, c], rr.at[it, c], r_send.at[it, k], r_recv.at[it, c], d, peer).start()
        if it < ITERS - 1:
            forward(it + 1)
        for k, peer in enumerate(c_peers):
            got = remote(
                rr.at[it, peer], rr.at[it, peer], r_send.at[it, k], r_recv.at[it, peer], d, peer
            )
            got.wait()
        row_sum = rr[it, 0]
        for k in range(1, n_cent):
            row_sum = row_sum + rr[it, k]
        u_old = uz[z] if it else jnp.ones((1, rows), jnp.float32)
        u_new = jnp.sqrt(u_old / row_sum)
        uz[z] = u_new
        if it < ITERS - 1:
            ucol[...] = to_column(u_new)
        for k, peer in enumerate(dp_peers):
            got = remote(
                cr.at[it, peer], cr.at[it, peer], c_send.at[it, k], c_recv.at[it, peer], peer, c
            )
            got.wait()
        col_sum = cr[it, 0]
        for k in range(1, n_dp):
            col_sum = col_sum + cr[it, k]
        v_old = vv[...] if it else jnp.ones((NB, block), jnp.float32)
        vv[...] = jnp.sqrt(v_old * ratio / col_sum)

    racc[...] = jnp.zeros_like(racc)

    @pl.loop(0, NB)
    def _(b):
        @pl.when(b == 5)
        def _():
            forward(0)

        at = pl.multiple_of(b * block, block)
        ch_b = rms_rows(cent[pl.ds(at, block), :])
        ch[pl.ds(at, block), :] = ch_b
        col = jnp.zeros((8, block), jnp.float32)
        for i in range(n_cent):
            part = slice(i * quarter, (i + 1) * quarter)
            s = lax.dot_general(
                xb[pl.ds(base + i * quarter, quarter), :], ch_b, NT,
                preferred_element_type=jnp.float32,
            )
            e = jnp.exp(s * scale)
            energy[b, part, :] = e
            racc[part, :] += lane_tiles(e)
            col = col + jnp.sum(e.reshape(quarter // 8, 8, block), axis=0)
        cr[0, d, pl.ds(b, 1), :] = jnp.sum(col, axis=0, keepdims=True)

    exchange(0)

    group = 64
    for it in range(1, ITERS):
        racc[...] = jnp.zeros_like(racc)

        @pl.loop(0, NB)
        def _(b):
            v_b = jnp.broadcast_to(vv[pl.ds(b, 1), :], (8, block))

            def step(g, col):
                r0 = pl.multiple_of(g * group, group)
                for i in range(group // 8):
                    e = energy[b, pl.ds(r0 + i * 8, 8), :]
                    u8 = ucol[pl.ds(r0 + i * 8, 8), :]
                    col = col + e * jnp.concatenate([u8] * (block // 128), axis=1)
                    racc[pl.ds(r0 + i * 8, 8), :] += lane_tiles(e * v_b)
                return col

            col = lax.fori_loop(0, rows // group, step, jnp.zeros((8, block), jnp.float32))
            cr[it, d, pl.ds(b, 1), :] = jnp.sum(col, axis=0, keepdims=True)

        exchange(it)

    def u_copy(k, owner):
        return remote(
            uz.at[owner], uz.at[owner], u_send.at[k], u_recv.at[owner], z_peers[k] * 2 + x, c
        )

    for k in range(n_z - 1):
        u_copy(k, z).start()
    forward(3)
    z_copy(z, first, z).wait_send()

    @pl.when(middle)
    def _():
        z_copy(z, 2 * z - first, n_z).wait_send()
        for src in order:
            relay(src).wait_send()

    for k, src in enumerate(order):
        k_copy(src, 0, c_core).wait()
        k_copy(src, 1, c_far).wait()
    for k in range(n_z - 1):
        u_copy(k, z_peers[k]).wait()
        src = z_peers[k]
        for i in range(n_cent):
            xb[pl.ds(pl.multiple_of(src * rows + i * quarter, quarter), quarter), :] = xg[
                src, i
            ].astype(jnp.bfloat16)

    def weigh(owner, s, dst):
        at = pl.multiple_of(owner * block + s * CHUNK, CHUNK)
        cc = ch[pl.ds(at, CHUNK), :]
        v_col = to_column(vv[pl.ds(owner, 1), :][:, s * CHUNK : (s + 1) * CHUNK])
        v_tile = jnp.concatenate([v_col] * (block // 128), axis=1)
        dst[s] = jnp.zeros((CHUNK, width), jnp.float32)

        def step(zz, acc):
            for h in range(rows // block):
                xr = xb[pl.ds(pl.multiple_of(zz * rows + h * block, block), block), :]
                u = uz[zz][:, h * block : (h + 1) * block]
                e = jnp.exp(
                    lax.dot_general(cc, xr, NT, preferred_element_type=jnp.float32) * scale
                )
                acc = acc + lane_tiles(e * u)
                q = ((total_cents * u) * e * v_tile).astype(jnp.bfloat16)
                dst[s] += jnp.dot(q, xr, preferred_element_type=jnp.float32)
            return acc

        acc = lax.fori_loop(0, n_z, step, jnp.zeros((CHUNK, 128), jnp.float32))
        return to_row(acc)

    n_s = block // CHUNK

    def w_copy(s):
        return remote(ws.at[s], wr.at[s], w_send.at[s], w_recv.at[s], d_x, c)

    for s in range(n_s):
        cfs[:, s * CHUNK : (s + 1) * CHUNK] = weigh(d_x, s, ws)
        w_copy(s).start()
    cf_copy = remote(cfs, cfr, w_send.at[n_s], w_recv.at[n_s], d_x, c)
    cf_copy.start()
    for s in range(n_s):
        out_m[:, s * CHUNK : (s + 1) * CHUNK] = weigh(d, s, out_w)
    for s in range(n_s):
        w_copy(s).wait()
        w = out_w[s] + wr[s]
        out_w[s] = w * lax.rsqrt(jnp.mean(w * w, axis=1, keepdims=True) + 1e-06)
    cf_copy.wait()
    out_m[...] = vv[pl.ds(d, 1), :] * (out_m[...] + cfr[...]) * (total_cents / total_rows)


def fused(embeddings, centroids):
    n_dp, n_cent = lax.axis_size("dp"), lax.axis_size("cent")
    rows, width = embeddings.shape
    cents = centroids.shape[0]
    n_z = n_dp // 2
    block = cents // NB
    quarter = rows // n_cent
    n_s = block // CHUNK
    f32 = jnp.float32
    dma = pltpu.SemaphoreType.DMA
    w, m = pl.pallas_call(
        functools.partial(
            kernel, float(rows * n_dp), float(cents * n_cent), n_dp, n_cent
        ),
        out_shape=(
            jax.ShapeDtypeStruct((n_s, CHUNK, width), f32),
            jax.ShapeDtypeStruct((1, block), f32),
        ),
        in_specs=[pl.BlockSpec(memory_space=pltpu.VMEM)] * 2,
        out_specs=(pl.BlockSpec(memory_space=pltpu.VMEM),) * 2,
        scratch_shapes=[
            pltpu.VMEM((NB, rows, block), f32),
            pltpu.VMEM((cents, width), jnp.bfloat16),
            pltpu.VMEM((n_z, n_cent, quarter, width), f32),
            pltpu.VMEM((n_z * rows, width), jnp.bfloat16),
            pltpu.VMEM((rows, 128), f32),
            pltpu.VMEM((rows, 128), f32),
            pltpu.VMEM((ITERS, n_dp, NB, block), f32),
            pltpu.VMEM((ITERS, n_cent, 1, rows), f32),
            pltpu.VMEM((n_z, 1, rows), f32),
            pltpu.VMEM((NB, block), f32),
            pltpu.VMEM((n_s, CHUNK, width), f32),
            pltpu.VMEM((n_s, CHUNK, width), f32),
            pltpu.VMEM((1, block), f32),
            pltpu.VMEM((1, block), f32),
            dma((ITERS, n_dp - 1)),
            dma((ITERS, n_dp)),
            dma((ITERS, n_cent - 1)),
            dma((ITERS, n_cent)),
            dma((n_z + 1,)),
            dma((n_z,)),
            dma((n_z,)),
            dma((n_z,)),
            dma((n_z, 2)),
            dma((n_z, 2)),
            dma((n_z - 1,)),
            dma((n_z,)),
            dma((n_s + 1,)),
            dma((n_s + 1,)),
        ],
        compiler_params=pltpu.CompilerParams(
            collective_id=0, has_side_effects=True, vmem_limit_bytes=60 * 2**20
        ),
    )(embeddings, centroids)
    return w.reshape(block, width), m.reshape(block)


def column_total(weights, energy):
    return lax.psum(jnp.dot(weights, energy, precision=lax.Precision.HIGHEST), "dp")


def local(embeddings, centroids):
    n_data = lax.axis_size("dp")
    xh = rms_rows(embeddings)
    ch = rms_rows(centroids)
    local_rows, width = xh.shape
    local_cents = ch.shape[0]
    total_rows = float(local_rows * n_data)
    total_cents = float(local_cents * lax.axis_size("cent"))
    scores = lax.dot_general(xh, ch, NT, preferred_element_type=jnp.float32)
    energy = jnp.exp(scores * (1.0 / (TAU * width)))
    u = jnp.ones((local_rows,), jnp.float32)
    v = jnp.ones((local_cents,), jnp.float32)
    for step_index in range(ITERS):
        rows_sum = lax.psum(jnp.dot(energy, v, precision=lax.Precision.HIGHEST), "cent")
        cols = column_total(u, energy)
        u, v = (jnp.sqrt(u / rows_sum), jnp.sqrt(v * (total_rows / total_cents) / cols))
    cols = column_total(u, energy)
    plan = (total_cents * u[:, None] * energy * v[None, :]).astype(jnp.bfloat16)
    share = local_cents // n_data
    weighted = lax.dot_general(
        plan, xh, (((0,), (0,)), ((), ())), preferred_element_type=jnp.float32
    )
    mine = lax.psum_scatter(weighted, "dp", scatter_dimension=0, tiled=True)
    mass_all = v * cols * (total_cents / total_rows)
    column_mass = lax.dynamic_slice_in_dim(mass_all, lax.axis_index("dp") * share, share, 0)
    new_centroids = mine * lax.rsqrt(jnp.mean(mine * mine, axis=1, keepdims=True) + 1e-06)
    return (new_centroids, column_mass)


def solution(mesh):
    in_specs = (P("dp", None), P("cent", None))
    out_specs = (P(("cent", "dp"), None), P(("cent", "dp")))
    small = mesh.shape["dp"] == NB and mesh.shape["cent"] == 4
    body = fused if small else local
    return jax.shard_map(body, mesh=mesh, in_specs=in_specs, out_specs=out_specs, check_vma=False)
```
